32 devices in a mesh: gx: 4 (over y, core), gy: 8 (over z, x).
Axes of the slice: x: 2, y: 2, z: 4, core: 2. Of those that a mesh axis runs over, the one named last changes fastest.
Arguments:
- patches: bfloat16 [33856, 768], P(('gx', 'gy')), may hold values from -6 to 6
- cotangent: bfloat16 [33856, 768], P(('gx', 'gy')), may hold values from -6 to 6
- counts: int32 [64], P(('gx', 'gy')), may hold values from 40 to 529, as said below
- blank_mask: int32 [64, 529], P(('gx', 'gy')), may hold values 0 or 1
- ln1_gain: bfloat16 [768], P(('gx', 'gy')), may hold values from 0.25 to 1.75
- ln1_shift: bfloat16 [768], P(('gx', 'gy')), may hold values from -1.75 to 1.75
- w_qkv: bfloat16 [768, 2304], P(('gx', 'gy')), may hold values from -0.21875 to 0.21875
- query_bias: bfloat16 [768], P(('gx', 'gy')), may hold values from -3 to 3
- value_bias: bfloat16 [768], P(('gx', 'gy')), may hold values from -0.3125 to 0.3125
- w_proj: bfloat16 [768, 768], P(('gx', 'gy')), may hold values from -1.75 to 1.75
- proj_bias: bfloat16 [768], P(('gx', 'gy')), may hold values from -1.75 to 1.75
- ln2_gain: bfloat16 [768], P(('gx', 'gy')), may hold values from 0.25 to 1.75
- ln2_shift: bfloat16 [768], P(('gx', 'gy')), may hold values from -1.75 to 1.75
- w_up: bfloat16 [768, 3072], P(('gx', 'gy')), may hold values from -0.21875 to 0.21875
- up_bias: bfloat16 [3072], P(('gx', 'gy')), may hold values from -3 to 3
- w_down: bfloat16 [3072, 768], P(('gx', 'gy')), may hold values from -0.109375 to 0.109375
- down_bias: bfloat16 [768], P(('gx', 'gy')), may hold values from -1.75 to 1.75
Outputs:
- out_patches: bfloat16 [33856, 768], P(('gx', 'gy'))
- grad_patches: bfloat16 [33856, 768], P(('gx', 'gy'))
- grad_ln1_gain: float32 [768], P(('gx', 'gy'))
- grad_ln1_shift: float32 [768], P(('gx', 'gy'))
- grad_w_qkv: float32 [768, 2304], P(('gx', 'gy'))
- grad_query_bias: float32 [768], P(('gx', 'gy'))
- grad_value_bias: float32 [768], P(('gx', 'gy'))
- grad_w_proj: float32 [768, 768], P(('gx', 'gy'))
- grad_proj_bias: float32 [768], P(('gx', 'gy'))
- grad_ln2_gain: float32 [768], P(('gx', 'gy'))
- grad_ln2_shift: float32 [768], P(('gx', 'gy'))
- grad_w_up: float32 [768, 3072], P(('gx', 'gy'))
- grad_up_bias: float32 [3072], P(('gx', 'gy'))
- grad_w_down: float32 [3072, 768], P(('gx', 'gy'))
- grad_down_bias: float32 [768], P(('gx', 'gy'))
The draws below stay inside these ranges and needn't reach their ends.
Inputs may be any that keep to these rules, and one draw needn't show every extreme that they name: `counts`: live patches of an item; one item has 529, another 529 // 13.
All inputs are finite; a program needn't handle non-finite values. No bound on the sum of `blank_mask` on one device may be relied on, other than what follows from the above.
Results may differ from the reference program's by a relative error of at most 0.013.
Values may be sent and summed in bfloat16 or wider, within the bound.
A program may use at most 192 MiB of HBM per device.

```python
import jax
import jax.numpy as jnp
from jax import lax

D = 768
HEADS = 12
HEAD_DIM = 64
FF = 3072
PATCHES = 529
ITEMS = 64
TOKENS = 33856


def draw_counts(key, part):
    first, second, third = jax.random.split(key, 3)
    values = jax.random.randint(first, (ITEMS,), PATCHES // 13, PATCHES + 1)
    largest_at = jax.random.randint(second, (), 0, ITEMS)
    least_at = (largest_at + 1 + jax.random.randint(third, (), 0, ITEMS - 1)) % ITEMS
    places = jnp.arange(ITEMS, dtype=jnp.int32)
    values = jnp.where(places == largest_at, PATCHES, values)
    values = jnp.where(places == least_at, PATCHES // 13, values)
    return values.astype(jnp.int32)


def place_ends(drawn, own_key, least, top_value):
    longest = drawn.shape.index(max(drawn.shape))
    spots = []
    for shift in (0, 1):
        where = [jax.random.randint(jax.random.fold_in(own_key, axis), (), 0, length) for axis, length in enumerate(drawn.shape)]
        where[longest] = (where[longest] + shift) % drawn.shape[longest]
        spots.append(tuple(where))
    return drawn.at[spots[0]].set(least).at[spots[1]].set(top_value)


def with_spikes(entries, stream_key, source, target, shards_of, factor):
    owner, partner = [(jnp.arange(entries.shape[axis_at]) // (entries.shape[axis_at] // shards_of)).reshape([-1 if axis == axis_at else 1 for axis in range(entries.ndim)]) for axis_at in (source, target)]
    chosen = jax.random.permutation(stream_key, shards_of)[partner]
    strong = (owner == chosen) | (owner == (partner + shards_of // 2) % shards_of)
    return jnp.where(strong, factor * entries, entries)


def level_of(rng, shape, cuts, least, top_value):
    def one(axis_at, parts):
        draws = jax.random.uniform(jax.random.fold_in(jax.random.fold_in(rng, 6), axis_at), (parts,), jnp.float32, least / len(cuts), top_value / len(cuts))
        return jnp.repeat(jnp.exp(draws), shape[axis_at] // parts).reshape((-1,) + (1,) * (len(shape) - axis_at - 1))

    level = one(*cuts[0])
    for cut in cuts[1:]:
        level = level * one(*cut)
    return level


def gaussian(stream_key, dims, deviation, limit, cuts=(), kind=jnp.bfloat16):
    drawn = jax.random.normal(stream_key, dims, jnp.float32) * deviation
    if len(cuts) > 0:
        drawn = level_of(stream_key, dims, cuts, -0.22, 0.18) * drawn
    return jnp.clip(drawn, min=-limit, max=limit).astype(kind)


def gaussian_with(stream_key, shape, scale, most, cuts, heavy, kind=jnp.bfloat16):
    drawn = scale * jax.random.normal(stream_key, shape, jnp.float32)
    if cuts:
        drawn = drawn * level_of(stream_key, shape, cuts, -0.22, 0.18)
    return jnp.clip(with_spikes(drawn, jax.random.fold_in(stream_key, 3), *heavy), -most, most).astype(kind)


def setup_inputs(seed: int = 0) -> dict:
    keys = jax.random.split(jax.random.key(seed), 18)
    return {
        "patches": gaussian(keys[0], (TOKENS, D), 1.0, 6.0, ((0, 32),)),
        "cotangent": gaussian_with(keys[1], (TOKENS, D), 1.0, 6.0, ((0, 32),), (0, 1, 32, 2.75)),
        "counts": draw_counts(jax.random.fold_in(keys[17], 71), 0),
        "blank_mask": place_ends((jax.random.randint(keys[3], (ITEMS, PATCHES), 0, 5) < 4).astype(jnp.int32), jax.random.fold_in(keys[3], 1), 0, 1),
        "ln1_gain": jnp.clip(1.0 + 0.15 * jax.random.normal(keys[4], (D,), jnp.float32), 0.25, 1.75).astype(jnp.bfloat16),
        "ln1_shift": gaussian(keys[5], (D,), 0.3, 1.75, ((0, 32),)),
        "w_qkv": gaussian(keys[6], (D, 3 * D), D ** -0.5, 0.21875, ((0, 32),)),
        "query_bias": gaussian(keys[7], (D,), 0.5, 3.0, ((0, 32),)),
        "value_bias": gaussian(keys[8], (D,), 0.05, 0.3125, ((0, 32),)),
        "w_proj": gaussian(keys[9], (D, D), (D // 64) ** -0.5, 1.75, ((0, 32),)),
        "proj_bias": gaussian(keys[10], (D,), 0.3, 1.75, ((0, 32),)),
        "ln2_gain": jnp.clip(1.0 + 0.15 * jax.random.normal(keys[11], (D,), jnp.float32), 0.25, 1.75).astype(jnp.bfloat16),
        "ln2_shift": gaussian(keys[12], (D,), 0.3, 1.75, ((0, 32),)),
        "w_up": gaussian(keys[13], (D, FF), D ** -0.5, 0.21875, ((0, 32),)),
        "up_bias": gaussian(keys[14], (FF,), 0.5, 3.0, ((0, 32),)),
        "w_down": gaussian(keys[15], (FF, D), FF ** -0.5, 0.109375, ((0, 32),)),
        "down_bias": gaussian(keys[16], (D,), 0.3, 1.75, ((0, 32),)),
    }


@jax.custom_vjp
def low(v):
    return lax.optimization_barrier(v.astype(jnp.bfloat16)).astype(jnp.float32)

@jax.custom_vjp
def low_back(v):
    return v

def low_keep(v):
    return (low(v), None)

def low_pass(kept, grad):
    return (grad,)

def back_keep(v):
    return (v, None)

def back_low(kept, grad):
    return (low(grad),)
low.defvjp(low_keep, low_pass)
low_back.defvjp(back_keep, back_low)
epsilon = 1e-06

def both_ways(tensor):
    return low_back(low(tensor))

def matmul(left, right):
    return jnp.dot(left, right, precision=lax.Precision.HIGHEST, preferred_element_type=jnp.float32)

def normalize(matrix, scales, shifts):
    centre = lax.optimization_barrier(jnp.mean(matrix, axis=-1, keepdims=True))
    centred = matrix - centre
    spread = lax.optimization_barrier(jnp.mean(centred * centred, axis=-1, keepdims=True))
    return centred * lax.rsqrt(spread + epsilon) * scales + shifts

def attend_item(queries, keys_all, values_all, allowed):
    length = queries.shape[0]
    split_q = queries.reshape(length, HEADS, HEAD_DIM)
    split_k = keys_all.reshape(length, HEADS, HEAD_DIM)
    split_v = values_all.reshape(length, HEADS, HEAD_DIM)
    raw = jnp.einsum('qhd,khd->hqk', split_q, split_k, precision=lax.Precision.HIGHEST)
    scores = low_back(raw * HEAD_DIM ** (-0.5))
    masked = jnp.where(allowed[None, None, :], scores, -1e+30)
    probs = jax.nn.softmax(masked, axis=-1)
    mixed_rows = jnp.einsum('hqk,khd->qhd', low(probs), split_v, precision=lax.Precision.HIGHEST)
    return mixed_rows.reshape(length, HEADS * HEAD_DIM)

def reference(patches, cotangent, counts, blank_mask, ln1_gain, ln1_shift, w_qkv, query_bias, value_bias, w_proj, proj_bias, ln2_gain, ln2_shift, w_up, up_bias, w_down, down_bias):
    positions = jnp.arange(PATCHES, dtype=jnp.int32)
    live_mask = positions[None, :] < counts[:, None]
    allowed = live_mask & ((blank_mask == 1) | (positions[None, :] == 0))
    live_rows = live_mask.reshape(-1, 1).astype(jnp.float32)
    checked = jax.checkpoint(attend_item)

    def one_item(pieces):
        return checked(pieces[0], pieces[1], pieces[2], pieces[3])

    def forward(inputs, gain_one, shift_one, qkv_weight, bias_query, bias_value, proj_weight, bias_proj, gain_two, shift_two, up_weight, bias_up, down_weight, bias_down):
        normed = low(normalize(inputs, gain_one, shift_one))
        projected = matmul(normed, low(qkv_weight))
        queries = both_ways(projected[:, :D] + bias_query)
        keys_all = both_ways(projected[:, D:2 * D])
        values_all = both_ways(projected[:, 2 * D:] + bias_value)
        stacked = (queries.reshape(ITEMS, PATCHES, D), keys_all.reshape(ITEMS, PATCHES, D), values_all.reshape(ITEMS, PATCHES, D), allowed)
        mixed_rows = both_ways(lax.map(one_item, stacked).reshape(TOKENS, D))
        branch = low_back(matmul(mixed_rows, low(proj_weight)) + bias_proj)
        residual = inputs + branch
        normed_two = low(normalize(residual, gain_two, shift_two))
        pre_act = low_back(matmul(normed_two, low(up_weight)) + bias_up)
        activated = low(jax.nn.gelu(pre_act, approximate=False))
        out_branch = low_back(matmul(activated, low(down_weight)) + bias_down)
        return (residual + out_branch) * live_rows
    floats = tuple((tensor.astype(jnp.float32) for tensor in (patches, ln1_gain, ln1_shift, w_qkv, query_bias, value_bias, w_proj, proj_bias, ln2_gain, ln2_shift, w_up, up_bias, w_down, down_bias)))
    output, pullback = jax.vjp(forward, *floats)
    grads = pullback(cotangent.astype(jnp.float32))
    return (output.astype(jnp.bfloat16), grads[0].astype(jnp.bfloat16), grads[1], grads[2], grads[3], grads[4], grads[5], grads[6], grads[7], grads[8], grads[9], grads[10], grads[11], grads[12], grads[13])
```

```python
from functools import partial

import jax
import jax.numpy as jnp
from jax import lax
from jax.experimental import pallas as pl
from jax.experimental.pallas import tpu as pltpu
from jax.sharding import PartitionSpec as P

HEAD_DIM = 64


epsilon = 1e-06


def normalize(matrix, scales, shifts):
    centre = jnp.mean(matrix, axis=-1, keepdims=True)
    centred = matrix - centre
    spread = jnp.mean(centred * centred, axis=-1, keepdims=True)
    return centred * lax.rsqrt(spread + epsilon) * scales + shifts


def split_heads(matrix):
    return matrix.reshape(matrix.shape[0], matrix.shape[1] // HEAD_DIM, HEAD_DIM)


def head_scores(queries, keys_all, allowed):
    raw = jnp.einsum(
        "qhd,khd->hqk",
        split_heads(queries),
        split_heads(keys_all),
        preferred_element_type=jnp.float32,
    )
    return jnp.where(allowed[None, None, :], raw * HEAD_DIM ** (-0.5), -1e30)


def attend_forward(pieces):
    queries, keys_all, values_all, allowed = pieces
    masked = head_scores(queries, keys_all, allowed)
    peak = jnp.max(masked, axis=-1, keepdims=True)
    log_total = peak + jnp.log(jnp.sum(jnp.exp(masked - peak), axis=-1, keepdims=True))
    probs = jnp.exp(masked - log_total)
    mixed_rows = jnp.einsum(
        "hqk,khd->qhd",
        probs.astype(jnp.bfloat16),
        split_heads(values_all),
        preferred_element_type=jnp.float32,
    )
    return (mixed_rows.reshape(queries.shape).astype(jnp.bfloat16), log_total)


def attend_backward(pieces):
    queries, keys_all, values_all, allowed, log_total, grad_mixed = pieces
    masked = head_scores(queries, keys_all, allowed)
    probs = jnp.exp(masked - log_total)
    grad_heads = split_heads(grad_mixed)
    grad_probs = jnp.einsum(
        "qhd,khd->hqk", grad_heads, split_heads(values_all), preferred_element_type=jnp.float32
    )
    inner = jnp.sum(grad_probs * probs, axis=-1, keepdims=True)
    grad_scores = (probs * (grad_probs - inner)).astype(jnp.bfloat16)
    scale_factor = HEAD_DIM ** (-0.5)
    grad_query = (
        jnp.einsum(
            "hqk,khd->qhd", grad_scores, split_heads(keys_all), preferred_element_type=jnp.float32
        )
        * scale_factor
    )
    grad_key = (
        jnp.einsum(
            "hqk,qhd->khd", grad_scores, split_heads(queries), preferred_element_type=jnp.float32
        )
        * scale_factor
    )
    grad_value = jnp.einsum(
        "hqk,qhd->khd", probs.astype(jnp.bfloat16), grad_heads, preferred_element_type=jnp.float32
    )
    joined = jnp.concatenate(
        [
            grad_query.reshape(queries.shape),
            grad_key.reshape(queries.shape),
            grad_value.reshape(queries.shape),
        ],
        axis=-1,
    )
    return joined.astype(jnp.bfloat16)


MESH = pl.DeviceIdType.MESH
ANY = pl.ANY


def gray(v):
    return v + (v // 2) * (1 - 2 * (v % 2))


class Place:
    def __init__(self):
        gx, gy = lax.axis_index("gx"), lax.axis_index("gy")
        self.y, self.c, self.z, self.x = gx // 2, gx % 2, gy // 2, gy % 2
        y, c, z, x = self.y, self.c, self.z, self.x
        self.p = gray(z)
        self.own = (y, x)
        self.first = (y + c * (1 - 2 * y), x + (1 - c) * (1 - 2 * x))
        self.second = (y + (1 - c) * (1 - 2 * y), x + c * (1 - 2 * x))
        self.far = (1 - y, 1 - x)
        self.to_first = self.dev(self.first, c, z)
        self.to_second = self.dev(self.second, c, z)
        self.to_next = self.dev(self.own, c, gray((self.p + 1) % 4))
        self.to_prev = self.dev(self.own, c, gray((self.p + 3) % 4))
        self.to_sibling = self.dev(self.own, 1 - c, z)

    def dev(self, yx, c, z):
        return (yx[0] * 2 + c, z * 2 + yx[1])

    def chip(self, back):
        return gray((self.p + 4 - back) % 4)

    def greet(self):
        barrier = pltpu.get_barrier_semaphore()
        peers = (self.to_first, self.to_second, self.to_next, self.to_prev, self.to_sibling)
        for peer in peers:
            pl.semaphore_signal(barrier, inc=1, device_id=peer, device_id_type=MESH)
        pl.semaphore_wait(barrier, len(peers))


class Gather:
    STAGES = 8

    def __init__(self, place, src, dst, send, recv, here):
        self.at, self.src, self.dst, self.send, self.recv, self.here = place, src, dst, send, recv, here

    def column(self, yx):
        return self.dst.at[yx[0], self.at.c, :, yx[1]]

    def remote(self, k, src, dst, device):
        return pltpu.make_async_remote_copy(
            src_ref=src, dst_ref=dst, send_sem=self.send.at[k], recv_sem=self.recv.at[k],
            device_id=device, device_id_type=MESH)

    def ring(self, k):
        a = self.at
        block = self.dst.at[a.y, a.c, a.chip(k), a.x]
        return self.remote(k, self.src if k == 0 else block, block, a.to_next)

    def first(self):
        col = self.column(self.at.own)
        return self.remote(3, col, col, self.at.to_first)

    def second(self, k):
        col = self.column(self.at.own if k == 0 else self.at.first)
        return self.remote(4 + k, col, col, self.at.to_second)

    def twin(self, k):
        a = self.at
        col = self.column((a.own, a.first, a.second, a.far)[k])
        return self.remote(6 + k, col, col, a.to_sibling)

    def local(self):
        a = self.at
        return pltpu.make_async_copy(self.src, self.dst.at[a.y, a.c, a.z, a.x], self.here)

    def stage(self, s):
        if s == 0:
            self.local().start()
            self.ring(0).start()
        elif s in (1, 2):
            self.ring(s - 1).wait_recv()
            self.ring(s).start()
        elif s == 3:
            self.local().wait()
            self.ring(2).wait_recv()
            self.first().start()
            self.second(0).start()
            self.twin(0).start()
        elif s == 4:
            self.first().wait_recv()
            self.second(1).start()
            self.twin(1).start()
        elif s == 5:
            self.second(0).wait_recv()
            self.twin(2).start()
        elif s == 6:
            self.second(1).wait_recv()
            self.twin(3).start()
        elif s == 7:
            for k in range(4):
                self.twin(k).wait_recv()

    def finish(self):
        for k in range(3):
            self.ring(k).wait_send()
        self.first().wait_send()
        self.second(0).wait_send()
        self.second(1).wait_send()
        for k in range(4):
            self.twin(k).wait_send()


def run_stages(jobs, offsets):
    last = max(o + j.STAGES for j, o in zip(jobs, offsets))
    for t in range(last):
        for job, o in zip(jobs, offsets):
            if 0 <= t - o < job.STAGES:
                job.stage(t - o)
    for job in jobs:
        job.finish()


def gather_all(shards, offsets):
    n = len(shards)

    def body(*refs):
        src, dst = refs[:n], refs[n:2 * n]
        send, recv, here = refs[2 * n:]
        place = Place()
        place.greet()
        jobs = [Gather(place, src[i], dst[i], send.at[i], recv.at[i], here.at[i]) for i in range(n)]
        run_stages(jobs, offsets)

    return pl.pallas_call(
        body,
        out_shape=[jax.ShapeDtypeStruct((2, 2, 4, 2) + s.shape, s.dtype) for s in shards],
        in_specs=[pl.BlockSpec(memory_space=ANY)] * n,
        out_specs=[pl.BlockSpec(memory_space=ANY)] * n,
        scratch_shapes=[pltpu.SemaphoreType.DMA((n, 10)), pltpu.SemaphoreType.DMA((n, 10)), pltpu.SemaphoreType.DMA((n,))],
        compiler_params=pltpu.CompilerParams(collective_id=0, has_side_effects=True),
        name="gather_weights",
    )(*shards)


class Scatter:
    STAGES = 9

    def __init__(self, place, src, out, held, twin, side, end, rings, send, recv, here):
        self.at, self.src, self.out = place, src, out
        self.held, self.twin, self.side, self.end, self.rings = held, twin, side, end, rings
        self.send, self.recv, self.here = send, recv, here

    def remote(self, k, src, dst, device):
        return pltpu.make_async_remote_copy(
            src_ref=src, dst_ref=dst, send_sem=self.send.at[k], recv_sem=self.recv.at[k],
            device_id=device, device_id_type=MESH)

    def load(self, k):
        a = self.at
        yx = (a.far, a.second, a.first, a.own)[k]
        return pltpu.make_async_copy(self.src.at[yx[0], a.c, :, yx[1]], self.held.at[k], self.here.at[k])

    def to_twin(self, k):
        a = self.at
        yx = (a.far, a.first, a.second, a.own)[k]
        return self.remote(k, self.src.at[yx[0], 1 - a.c, :, yx[1]], self.twin.at[k], a.to_sibling)

    def to_second(self, k):
        return self.remote(4 + k, self.held.at[k], self.side.at[k], self.at.to_second)

    def to_first(self):
        return self.remote(6, self.held.at[2], self.end, self.at.to_first)

    def ring(self, k):
        return self.remote(7 + k, self.held.at[3, self.at.chip(k + 1)], self.rings.at[k], self.at.to_next)

    def add(self, k, other):
        held = self.held

        def one(z, carry):
            total = held[k, z].astype(jnp.float32) + other[z].astype(jnp.float32)
            held[k, z] = total.astype(held.dtype)
            return carry

        lax.fori_loop(0, 4, one, 0)

    def stage(self, s):
        a = self.at
        if s == 0:
            for k in range(4):
                self.load(k).start()
                self.to_twin(k).start()
        elif s == 1:
            for k in range(2):
                self.load(k).wait()
                self.to_twin(k).wait_recv()
                self.add(k, self.twin.at[k])
                self.to_second(k).start()
        elif s == 2:
            for k in (2, 3):
                self.load(k).wait()
                self.to_twin(k).wait_recv()
                self.add(k, self.twin.at[k])
        elif s == 3:
            self.to_second(0).wait_recv()
            self.add(2, self.side.at[0])
            self.to_first().start()
        elif s == 4:
            self.to_second(1).wait_recv()
            self.add(3, self.side.at[1])
        elif s == 5:
            self.to_first().wait_recv()
            self.add(3, self.end)
            self.ring(0).start()
        elif s in (6, 7):
            self.ring(s - 6).wait_recv()
            z = a.chip(s - 4)
            total = self.held[3, z].astype(jnp.float32) + self.rings[s - 6].astype(jnp.float32)
            self.held[3, z] = total.astype(self.held.dtype)
            self.ring(s - 5).start()
        elif s == 8:
            self.ring(2).wait_recv()
            self.out[...] = self.held[3, a.z].astype(jnp.float32) + self.rings[2].astype(jnp.float32)

    def finish(self):
        for k in range(4):
            self.to_twin(k).wait_send()
        self.to_second(0).wait_send()
        self.to_second(1).wait_send()
        self.to_first().wait_send()
        for k in range(3):
            self.ring(k).wait_send()


def scatter_scratch(rows, cols, dtype):
    return [pltpu.VMEM((4, 4, rows, cols), dtype), pltpu.VMEM((4, 4, rows, cols), dtype),
            pltpu.VMEM((2, 4, rows, cols), dtype), pltpu.VMEM((4, rows, cols), dtype),
            pltpu.VMEM((3, rows, cols), dtype)]


def scatter_all(partials, offsets):
    n = len(partials)

    def body(*refs):
        src, out = refs[:n], refs[n:2 * n]
        scratch = refs[2 * n:7 * n]
        send, recv, here = refs[7 * n:]
        place = Place()
        place.greet()
        jobs = [Scatter(place, src[i], out[i], *scratch[5 * i:5 * i + 5], send.at[i], recv.at[i], here.at[i]) for i in range(n)]
        run_stages(jobs, offsets)

    scratch = []
    for p in partials:
        scratch += scatter_scratch(*p.shape[4:], p.dtype)
    return pl.pallas_call(
        body,
        out_shape=[jax.ShapeDtypeStruct(p.shape[4:], jnp.float32) for p in partials],
        in_specs=[pl.BlockSpec(memory_space=ANY)] * n,
        out_specs=[pl.BlockSpec(memory_space=pltpu.VMEM)] * n,
        scratch_shapes=scratch + [pltpu.SemaphoreType.DMA((n, 10)), pltpu.SemaphoreType.DMA((n, 10)), pltpu.SemaphoreType.DMA((n, 4))],
        compiler_params=pltpu.CompilerParams(collective_id=1, has_side_effects=True, vmem_limit_bytes=50 << 20),
        name="scatter_grads",
    )(*partials)

def pack_vectors(eight, wide):
    block = jnp.stack(eight, axis=-2)
    rows = wide.reshape(wide.shape[:-1] + (4, -1))
    lead = [(0, 0)] * (block.ndim - 2)
    rows = jnp.pad(rows, lead + [(0, 4), (0, 0)])
    joined = jnp.concatenate([block, rows], axis=-1)
    return jnp.pad(joined, lead + [(0, 0), (0, 128 - joined.shape[-1])])


def unpack_vectors(blocks, share):
    eight = tuple(blocks[:, k, :share].reshape(-1) for k in range(8))
    return eight, blocks[:, :4, share : 2 * share].reshape(-1)


def local(
    patches,
    cotangent,
    counts,
    blank_mask,
    ln1_gain,
    ln1_shift,
    w_qkv,
    query_bias,
    value_bias,
    w_proj,
    proj_bias,
    ln2_gain,
    ln2_shift,
    w_up,
    up_bias,
    w_down,
    down_bias,
):
    items_here = counts.shape[0]
    length = blank_mask.shape[1]
    width = patches.shape[1]
    positions = jnp.arange(length, dtype=jnp.int32)
    live_mask = positions[None, :] < counts[:, None]
    allowed = live_mask & ((blank_mask == 1) | (positions[None, :] == 0))
    live_rows = live_mask.reshape(-1, 1).astype(jnp.float32)
    vectors = pack_vectors(
        (ln1_gain, ln1_shift, query_bias, value_bias, proj_bias, ln2_gain, ln2_shift, down_bias),
        up_bias,
    )
    all_qkv, all_vectors, all_proj, all_up, all_down = gather_all(
        (w_qkv, vectors, w_proj, w_up, w_down), (0, 0, 3, 4, 7)
    )
    qkv_weight = all_qkv.reshape(width, -1)
    proj_weight = all_proj.reshape(width, width)
    up_weight = all_up.reshape(width, -1)
    down_weight = all_down.reshape(-1, width)
    (
        gain_one,
        shift_one,
        bias_query,
        bias_value,
        bias_proj,
        gain_two,
        shift_two,
        bias_down,
    ), bias_up = unpack_vectors(all_vectors.reshape(-1, 8, 128), w_qkv.shape[0])
    inputs = patches.astype(jnp.float32)
    gain_float = gain_one.astype(jnp.float32)
    shift_float = shift_one.astype(jnp.float32)
    normed_low = normalize(inputs, gain_float, shift_float).astype(jnp.bfloat16)
    projected = jnp.dot(normed_low, qkv_weight, preferred_element_type=jnp.float32)
    queries = (projected[:, :width] + bias_query.astype(jnp.float32)).astype(jnp.bfloat16)
    keys_all = projected[:, width : 2 * width].astype(jnp.bfloat16)
    values_all = (projected[:, 2 * width :] + bias_value.astype(jnp.float32)).astype(jnp.bfloat16)
    per_item = (
        queries.reshape(items_here, length, width),
        keys_all.reshape(items_here, length, width),
        values_all.reshape(items_here, length, width),
        allowed,
    )
    mixed_items, log_totals = lax.map(attend_forward, per_item)
    mixed_low = mixed_items.reshape(-1, width)
    residual = (
        inputs
        + jnp.dot(mixed_low, proj_weight, preferred_element_type=jnp.float32)
        + bias_proj.astype(jnp.float32)
    )
    normed_two = normalize(
        residual, gain_two.astype(jnp.float32), shift_two.astype(jnp.float32)
    ).astype(jnp.bfloat16)
    pre_act = jnp.dot(normed_two, up_weight, preferred_element_type=jnp.float32) + bias_up.astype(
        jnp.float32
    )
    activated, gelu_back = jax.vjp(partial(jax.nn.gelu, approximate=False), pre_act)
    act_low = activated.astype(jnp.bfloat16)
    out_branch = jnp.dot(
        act_low, down_weight, preferred_element_type=jnp.float32
    ) + bias_down.astype(jnp.float32)
    output = ((residual + out_branch) * live_rows).astype(jnp.bfloat16)
    grad_out = cotangent.astype(jnp.float32) * live_rows
    grad_down_low = grad_out.astype(jnp.bfloat16)
    down_grad = jnp.einsum("tf,td->fd", act_low, grad_down_low, preferred_element_type=jnp.float32)
    down_bias_grad = jnp.sum(grad_down_low.astype(jnp.float32), axis=0)
    grad_act = jnp.einsum(
        "td,fd->tf", grad_down_low, down_weight, preferred_element_type=jnp.float32
    )
    grad_pre_low = gelu_back(grad_act)[0].astype(jnp.bfloat16)
    up_grad = jnp.einsum("td,tf->df", normed_two, grad_pre_low, preferred_element_type=jnp.float32)
    up_bias_grad = jnp.sum(grad_pre_low.astype(jnp.float32), axis=0)
    grad_normed_two = jnp.einsum(
        "tf,df->td", grad_pre_low, up_weight, preferred_element_type=jnp.float32
    )
    _, norm_back_two = jax.vjp(
        normalize, residual, gain_two.astype(jnp.float32), shift_two.astype(jnp.float32)
    )
    grad_resid_part, gain_two_grad, shift_two_grad = norm_back_two(grad_normed_two)
    grad_resid = grad_out + grad_resid_part
    grad_branch_low = grad_resid.astype(jnp.bfloat16)
    proj_grad = jnp.einsum(
        "td,te->de", mixed_low, grad_branch_low, preferred_element_type=jnp.float32
    )
    proj_bias_grad = jnp.sum(grad_branch_low.astype(jnp.float32), axis=0)
    grad_mixed = jnp.einsum(
        "te,de->td", grad_branch_low, proj_weight, preferred_element_type=jnp.float32
    ).astype(jnp.bfloat16)
    back_items = (
        per_item[0],
        per_item[1],
        per_item[2],
        allowed,
        log_totals,
        grad_mixed.reshape(items_here, length, width),
    )
    grad_projected = lax.map(attend_backward, back_items).reshape(-1, 3 * width)
    qkv_grad = jnp.einsum(
        "td,te->de", normed_low, grad_projected, preferred_element_type=jnp.float32
    )
    query_bias_grad = jnp.sum(grad_projected[:, :width].astype(jnp.float32), axis=0)
    value_bias_grad = jnp.sum(grad_projected[:, 2 * width :].astype(jnp.float32), axis=0)
    grad_normed = jnp.einsum(
        "te,de->td", grad_projected, qkv_weight, preferred_element_type=jnp.float32
    )
    _, norm_back_one = jax.vjp(
        normalize, inputs, gain_one.astype(jnp.float32), shift_one.astype(jnp.float32)
    )
    grad_input_part, gain_one_grad, shift_one_grad = norm_back_one(grad_normed)
    grad_input = (grad_resid + grad_input_part).astype(jnp.bfloat16)
    packed = pack_vectors(
        tuple(
            v.reshape(-1, w_qkv.shape[0])
            for v in (
                gain_one_grad,
                shift_one_grad,
                query_bias_grad,
                value_bias_grad,
                proj_bias_grad,
                gain_two_grad,
                shift_two_grad,
                down_bias_grad,
            )
        ),
        up_bias_grad.reshape(-1, up_bias.shape[0]),
    )
    low = jnp.bfloat16
    blocks = tuple(
        t.reshape((2, 2, 4, 2) + s)
        for t, s in (
            (down_grad.astype(low), w_down.shape),
            (up_grad.astype(low), w_up.shape),
            (proj_grad.astype(low), w_proj.shape),
            (qkv_grad.astype(low), w_qkv.shape),
            (packed, (8, 128)),
        )
    )
    own_down, own_up, own_proj, own_qkv, own_packed = scatter_all(blocks, (0, 3, 6, 7, 8))
    own_vectors, own_up_bias = unpack_vectors(own_packed[None], w_qkv.shape[0])
    return (
        output,
        grad_input,
        own_vectors[0],
        own_vectors[1],
        own_qkv,
        own_vectors[2],
        own_vectors[3],
        own_proj,
        own_vectors[4],
        own_vectors[5],
        own_vectors[6],
        own_up,
        own_up_bias,
        own_down,
        own_vectors[7],
    )


def plain_local(
    patches,
    cotangent,
    counts,
    blank_mask,
    ln1_gain,
    ln1_shift,
    w_qkv,
    query_bias,
    value_bias,
    w_proj,
    proj_bias,
    ln2_gain,
    ln2_shift,
    w_up,
    up_bias,
    w_down,
    down_bias,
):
    items_here = counts.shape[0]
    length = blank_mask.shape[1]
    width = patches.shape[1]
    positions = jnp.arange(length, dtype=jnp.int32)
    live_mask = positions[None, :] < counts[:, None]
    allowed = live_mask & ((blank_mask == 1) | (positions[None, :] == 0))
    live_rows = live_mask.reshape(-1, 1).astype(jnp.float32)
    attn_full = (
        lax.all_gather(ln1_gain, ("gx", "gy"), axis=0, tiled=True),
        lax.all_gather(ln1_shift, ("gx", "gy"), axis=0, tiled=True),
        lax.all_gather(w_qkv, ("gx", "gy"), axis=0, tiled=True),
        lax.all_gather(query_bias, ("gx", "gy"), axis=0, tiled=True),
        lax.all_gather(value_bias, ("gx", "gy"), axis=0, tiled=True),
        lax.all_gather(w_proj, ("gx", "gy"), axis=0, tiled=True),
        lax.all_gather(proj_bias, ("gx", "gy"), axis=0, tiled=True),
    )
    gain_one, shift_one, qkv_weight, bias_query, bias_value, proj_weight, bias_proj = attn_full
    inputs = patches.astype(jnp.float32)
    gain_float = gain_one.astype(jnp.float32)
    shift_float = shift_one.astype(jnp.float32)
    normed_low = normalize(inputs, gain_float, shift_float).astype(jnp.bfloat16)
    projected = jnp.dot(normed_low, qkv_weight, preferred_element_type=jnp.float32)
    queries = (projected[:, :width] + bias_query.astype(jnp.float32)).astype(jnp.bfloat16)
    keys_all = projected[:, width : 2 * width].astype(jnp.bfloat16)
    values_all = (projected[:, 2 * width :] + bias_value.astype(jnp.float32)).astype(jnp.bfloat16)
    per_item = (
        queries.reshape(items_here, length, width),
        keys_all.reshape(items_here, length, width),
        values_all.reshape(items_here, length, width),
        allowed,
    )
    mixed_items, log_totals = lax.map(attend_forward, per_item)
    mixed_low = mixed_items.reshape(-1, width)
    residual = (
        inputs
        + jnp.dot(mixed_low, proj_weight, preferred_element_type=jnp.float32)
        + bias_proj.astype(jnp.float32)
    )
    mlp_full = (
        lax.all_gather(ln2_gain, ("gx", "gy"), axis=0, tiled=True),
        lax.all_gather(ln2_shift, ("gx", "gy"), axis=0, tiled=True),
        lax.all_gather(w_up, ("gx", "gy"), axis=0, tiled=True),
        lax.all_gather(up_bias, ("gx", "gy"), axis=0, tiled=True),
        lax.all_gather(w_down, ("gx", "gy"), axis=0, tiled=True),
        lax.all_gather(down_bias, ("gx", "gy"), axis=0, tiled=True),
    )
    gain_two, shift_two, up_weight, bias_up, down_weight, bias_down = mlp_full
    normed_two = normalize(
        residual, gain_two.astype(jnp.float32), shift_two.astype(jnp.float32)
    ).astype(jnp.bfloat16)
    pre_act = jnp.dot(normed_two, up_weight, preferred_element_type=jnp.float32) + bias_up.astype(
        jnp.float32
    )
    activated, gelu_back = jax.vjp(partial(jax.nn.gelu, approximate=False), pre_act)
    act_low = activated.astype(jnp.bfloat16)
    out_branch = jnp.dot(
        act_low, down_weight, preferred_element_type=jnp.float32
    ) + bias_down.astype(jnp.float32)
    output = ((residual + out_branch) * live_rows).astype(jnp.bfloat16)
    mlp_back = (
        lax.all_gather(ln2_gain, ("gx", "gy"), axis=0, tiled=True),
        lax.all_gather(ln2_shift, ("gx", "gy"), axis=0, tiled=True),
        lax.all_gather(w_up, ("gx", "gy"), axis=0, tiled=True),
        lax.all_gather(up_bias, ("gx", "gy"), axis=0, tiled=True),
        lax.all_gather(w_down, ("gx", "gy"), axis=0, tiled=True),
        lax.all_gather(down_bias, ("gx", "gy"), axis=0, tiled=True),
    )
    gain_two_b, shift_two_b, up_weight_b, bias_up_b, down_weight_b, bias_down_b = mlp_back
    grad_out = cotangent.astype(jnp.float32) * live_rows
    grad_down_low = grad_out.astype(jnp.bfloat16)
    down_grad = jnp.einsum("tf,td->fd", act_low, grad_down_low, preferred_element_type=jnp.float32)
    down_bias_grad = jnp.sum(grad_down_low.astype(jnp.float32), axis=0)
    grad_act = jnp.einsum(
        "td,fd->tf", grad_down_low, down_weight_b, preferred_element_type=jnp.float32
    )
    grad_pre_low = gelu_back(grad_act)[0].astype(jnp.bfloat16)
    up_grad = jnp.einsum("td,tf->df", normed_two, grad_pre_low, preferred_element_type=jnp.float32)
    up_bias_grad = jnp.sum(grad_pre_low.astype(jnp.float32), axis=0)
    grad_normed_two = jnp.einsum(
        "tf,df->td", grad_pre_low, up_weight_b, preferred_element_type=jnp.float32
    )
    _, norm_back_two = jax.vjp(
        normalize, residual, gain_two_b.astype(jnp.float32), shift_two_b.astype(jnp.float32)
    )
    grad_resid_part, gain_two_grad, shift_two_grad = norm_back_two(grad_normed_two)
    grad_resid = grad_out + grad_resid_part
    mlp_owned = (
        lax.psum_scatter(gain_two_grad, ("gx", "gy"), scatter_dimension=0, tiled=True),
        lax.psum_scatter(shift_two_grad, ("gx", "gy"), scatter_dimension=0, tiled=True),
        lax.psum_scatter(up_grad, ("gx", "gy"), scatter_dimension=0, tiled=True),
        lax.psum_scatter(up_bias_grad, ("gx", "gy"), scatter_dimension=0, tiled=True),
        lax.psum_scatter(down_grad, ("gx", "gy"), scatter_dimension=0, tiled=True),
        lax.psum_scatter(down_bias_grad, ("gx", "gy"), scatter_dimension=0, tiled=True),
    )
    attn_back = (
        lax.all_gather(ln1_gain, ("gx", "gy"), axis=0, tiled=True),
        lax.all_gather(ln1_shift, ("gx", "gy"), axis=0, tiled=True),
        lax.all_gather(w_qkv, ("gx", "gy"), axis=0, tiled=True),
        lax.all_gather(query_bias, ("gx", "gy"), axis=0, tiled=True),
        lax.all_gather(value_bias, ("gx", "gy"), axis=0, tiled=True),
        lax.all_gather(w_proj, ("gx", "gy"), axis=0, tiled=True),
        lax.all_gather(proj_bias, ("gx", "gy"), axis=0, tiled=True),
    )
    (
        gain_one_b,
        shift_one_b,
        qkv_weight_b,
        bias_query_b,
        bias_value_b,
        proj_weight_b,
        bias_proj_b,
    ) = attn_back
    grad_branch_low = grad_resid.astype(jnp.bfloat16)
    proj_grad = jnp.einsum(
        "td,te->de", mixed_low, grad_branch_low, preferred_element_type=jnp.float32
    )
    proj_bias_grad = jnp.sum(grad_branch_low.astype(jnp.float32), axis=0)
    grad_mixed = jnp.einsum(
        "te,de->td", grad_branch_low, proj_weight_b, preferred_element_type=jnp.float32
    ).astype(jnp.bfloat16)
    back_items = (
        per_item[0],
        per_item[1],
        per_item[2],
        allowed,
        log_totals,
        grad_mixed.reshape(items_here, length, width),
    )
    grad_projected = lax.map(attend_backward, back_items).reshape(-1, 3 * width)
    qkv_grad = jnp.einsum(
        "td,te->de", normed_low, grad_projected, preferred_element_type=jnp.float32
    )
    query_bias_grad = jnp.sum(grad_projected[:, :width].astype(jnp.float32), axis=0)
    value_bias_grad = jnp.sum(grad_projected[:, 2 * width :].astype(jnp.float32), axis=0)
    grad_normed = jnp.einsum(
        "te,de->td", grad_projected, qkv_weight_b, preferred_element_type=jnp.float32
    )
    _, norm_back_one = jax.vjp(
        normalize, inputs, gain_one_b.astype(jnp.float32), shift_one_b.astype(jnp.float32)
    )
    grad_input_part, gain_one_grad, shift_one_grad = norm_back_one(grad_normed)
    grad_input = (grad_resid + grad_input_part).astype(jnp.bfloat16)
    attn_owned = (
        lax.psum_scatter(gain_one_grad, ("gx", "gy"), scatter_dimension=0, tiled=True),
        lax.psum_scatter(shift_one_grad, ("gx", "gy"), scatter_dimension=0, tiled=True),
        lax.psum_scatter(qkv_grad, ("gx", "gy"), scatter_dimension=0, tiled=True),
        lax.psum_scatter(query_bias_grad, ("gx", "gy"), scatter_dimension=0, tiled=True),
        lax.psum_scatter(value_bias_grad, ("gx", "gy"), scatter_dimension=0, tiled=True),
        lax.psum_scatter(proj_grad, ("gx", "gy"), scatter_dimension=0, tiled=True),
        lax.psum_scatter(proj_bias_grad, ("gx", "gy"), scatter_dimension=0, tiled=True),
    )
    owned_all = attn_owned + mlp_owned
    return (
        output,
        grad_input,
        owned_all[0],
        owned_all[1],
        owned_all[2],
        owned_all[3],
        owned_all[4],
        owned_all[5],
        owned_all[6],
        owned_all[7],
        owned_all[8],
        owned_all[9],
        owned_all[10],
        owned_all[11],
        owned_all[12],
    )


def solution(mesh):
    placed = (
        P(("gx", "gy"), None),
        P(("gx", "gy"), None),
        P(("gx", "gy")),
        P(("gx", "gy"), None),
        P(("gx", "gy")),
        P(("gx", "gy")),
        P(("gx", "gy"), None),
        P(("gx", "gy")),
        P(("gx", "gy")),
        P(("gx", "gy"), None),
        P(("gx", "gy")),
        P(("gx", "gy")),
        P(("gx", "gy")),
        P(("gx", "gy"), None),
        P(("gx", "gy")),
        P(("gx", "gy"), None),
        P(("gx", "gy")),
    )
    mine = dict(mesh.shape) == {"gx": 4, "gy": 8}
    return jax.shard_map(
        local if mine else plain_local,
        mesh=mesh,
        in_specs=placed,
        out_specs=(
            P(("gx", "gy"), None),
            P(("gx", "gy"), None),
            P(("gx", "gy")),
            P(("gx", "gy")),
            P(("gx", "gy"), None),
            P(("gx", "gy")),
            P(("gx", "gy")),
            P(("gx", "gy"), None),
            P(("gx", "gy")),
            P(("gx", "gy")),
            P(("gx", "gy")),
            P(("gx", "gy"), None),
            P(("gx", "gy")),
            P(("gx", "gy"), None),
            P(("gx", "gy")),
        ),
        check_vma=False,
    )
```

```python
import functools
from functools import partial

import jax
import jax.numpy as jnp
from jax import lax
from jax.experimental import pallas as pl
from jax.experimental.pallas import tpu as pltpu
from jax.sharding import PartitionSpec as P

HEAD_DIM = 64


epsilon = 1e-06


def normalize(matrix, scales, shifts):
    centre = jnp.mean(matrix, axis=-1, keepdims=True)
    centred = matrix - centre
    spread = jnp.mean(centred * centred, axis=-1, keepdims=True)
    return centred * lax.rsqrt(spread + epsilon) * scales + shifts


def split_heads(matrix):
    return matrix.reshape(matrix.shape[0], matrix.shape[1] // HEAD_DIM, HEAD_DIM)


def head_scores(queries, keys_all, allowed):
    raw = jnp.einsum(
        "qhd,khd->hqk",
        split_heads(queries),
        split_heads(keys_all),
        preferred_element_type=jnp.float32,
    )
    return jnp.where(allowed[None, None, :], raw * HEAD_DIM ** (-0.5), -1e30)


def attend_forward(pieces):
    queries, keys_all, values_all, allowed = pieces
    masked = head_scores(queries, keys_all, allowed)
    peak = jnp.max(masked, axis=-1, keepdims=True)
    log_total = peak + jnp.log(jnp.sum(jnp.exp(masked - peak), axis=-1, keepdims=True))
    probs = jnp.exp(masked - log_total)
    mixed_rows = jnp.einsum(
        "hqk,khd->qhd",
        probs.astype(jnp.bfloat16),
        split_heads(values_all),
        preferred_element_type=jnp.float32,
    )
    return (mixed_rows.reshape(queries.shape).astype(jnp.bfloat16), log_total)


def attend_backward(pieces):
    queries, keys_all, values_all, allowed, log_total, grad_mixed = pieces
    masked = head_scores(queries, keys_all, allowed)
    probs = jnp.exp(masked - log_total)
    grad_heads = split_heads(grad_mixed)
    grad_probs = jnp.einsum(
        "qhd,khd->hqk", grad_heads, split_heads(values_all), preferred_element_type=jnp.float32
    )
    inner = jnp.sum(grad_probs * probs, axis=-1, keepdims=True)
    grad_scores = (probs * (grad_probs - inner)).astype(jnp.bfloat16)
    scale_factor = HEAD_DIM ** (-0.5)
    grad_query = (
        jnp.einsum(
            "hqk,khd->qhd", grad_scores, split_heads(keys_all), preferred_element_type=jnp.float32
        )
        * scale_factor
    )
    grad_key = (
        jnp.einsum(
            "hqk,qhd->khd", grad_scores, split_heads(queries), preferred_element_type=jnp.float32
        )
        * scale_factor
    )
    grad_value = jnp.einsum(
        "hqk,qhd->khd", probs.astype(jnp.bfloat16), grad_heads, preferred_element_type=jnp.float32
    )
    joined = jnp.concatenate(
        [
            grad_query.reshape(queries.shape),
            grad_key.reshape(queries.shape),
            grad_value.reshape(queries.shape),
        ],
        axis=-1,
    )
    return joined.astype(jnp.bfloat16)


MESH = pl.DeviceIdType.MESH
ANY = pl.ANY


def gray(v):
    return v + (v // 2) * (1 - 2 * (v % 2))


class Place:
    def __init__(self):
        gx, gy = lax.axis_index("gx"), lax.axis_index("gy")
        self.y, self.c, self.z, self.x = gx // 2, gx % 2, gy // 2, gy % 2
        y, c, z, x = self.y, self.c, self.z, self.x
        self.p = gray(z)
        self.own = (y, x)
        self.first = (y + c * (1 - 2 * y), x + (1 - c) * (1 - 2 * x))
        self.second = (y + (1 - c) * (1 - 2 * y), x + c * (1 - 2 * x))
        self.far = (1 - y, 1 - x)
        self.to_first = self.dev(self.first, c, z)
        self.to_second = self.dev(self.second, c, z)
        self.to_next = self.dev(self.own, c, gray((self.p + 1) % 4))
        self.to_prev = self.dev(self.own, c, gray((self.p + 3) % 4))
        self.to_sibling = self.dev(self.own, 1 - c, z)

    def dev(self, yx, c, z):
        return (yx[0] * 2 + c, z * 2 + yx[1])

    def chip(self, back):
        return gray((self.p + 4 - back) % 4)

    def greet(self):
        barrier = pltpu.get_barrier_semaphore()
        peers = (self.to_first, self.to_second, self.to_next, self.to_prev, self.to_sibling)
        for peer in peers:
            pl.semaphore_signal(barrier, inc=1, device_id=peer, device_id_type=MESH)
        pl.semaphore_wait(barrier, len(peers))


class Gather:
    STAGES = 8

    def __init__(self, place, src, dst, send, recv, here):
        self.at, self.src, self.dst, self.send, self.recv, self.here = place, src, dst, send, recv, here

    def column(self, yx):
        return self.dst.at[yx[0], self.at.c, :, yx[1]]

    def remote(self, k, src, dst, device):
        return pltpu.make_async_remote_copy(
            src_ref=src, dst_ref=dst, send_sem=self.send.at[k], recv_sem=self.recv.at[k],
            device_id=device, device_id_type=MESH)

    def ring(self, k):
        a = self.at
        block = self.dst.at[a.y, a.c, a.chip(k), a.x]
        return self.remote(k, self.src if k == 0 else block, block, a.to_next)

    def first(self):
        col = self.column(self.at.own)
        return self.remote(3, col, col, self.at.to_first)

    def second(self, k):
        col = self.column(self.at.own if k == 0 else self.at.first)
        return self.remote(4 + k, col, col, self.at.to_second)

    def twin(self, k):
        a = self.at
        col = self.column((a.own, a.first, a.second, a.far)[k])
        return self.remote(6 + k, col, col, a.to_sibling)

    def local(self):
        a = self.at
        return pltpu.make_async_copy(self.src, self.dst.at[a.y, a.c, a.z, a.x], self.here)

    def stage(self, s):
        if s == 0:
            self.local().start()
            self.ring(0).start()
        elif s in (1, 2):
            self.ring(s - 1).wait_recv()
            self.ring(s).start()
        elif s == 3:
            self.local().wait()
            self.ring(2).wait_recv()
            self.first().start()
            self.second(0).start()
            self.twin(0).start()
        elif s == 4:
            self.first().wait_recv()
            self.second(1).start()
            self.twin(1).start()
        elif s == 5:
            self.second(0).wait_recv()
            self.twin(2).start()
        elif s == 6:
            self.second(1).wait_recv()
            self.twin(3).start()
        elif s == 7:
            for k in range(4):
                self.twin(k).wait_recv()

    def finish(self):
        for k in range(3):
            self.ring(k).wait_send()
        self.first().wait_send()
        self.second(0).wait_send()
        self.second(1).wait_send()
        for k in range(4):
            self.twin(k).wait_send()


def run_stages(jobs, offsets):
    last = max(o + j.STAGES for j, o in zip(jobs, offsets))
    for t in range(last):
        for job, o in zip(jobs, offsets):
            if 0 <= t - o < job.STAGES:
                job.stage(t - o)
    for job in jobs:
        job.finish()


def gather_all(shards, offsets):
    n = len(shards)

    def body(*refs):
        src, dst = refs[:n], refs[n:2 * n]
        send, recv, here = refs[2 * n:]
        place = Place()
        place.greet()
        jobs = [Gather(place, src[i], dst[i], send.at[i], recv.at[i], here.at[i]) for i in range(n)]
        run_stages(jobs, offsets)

    return pl.pallas_call(
        body,
        out_shape=[jax.ShapeDtypeStruct((2, 2, 4, 2) + s.shape, s.dtype) for s in shards],
        in_specs=[pl.BlockSpec(memory_space=ANY)] * n,
        out_specs=[pl.BlockSpec(memory_space=ANY)] * n,
        scratch_shapes=[pltpu.SemaphoreType.DMA((n, 10)), pltpu.SemaphoreType.DMA((n, 10)), pltpu.SemaphoreType.DMA((n,))],
        compiler_params=pltpu.CompilerParams(collective_id=0, has_side_effects=True),
        name="gather_weights",
    )(*shards)


class Scatter:
    STAGES = 9

    def __init__(self, place, src, out, held, twin, side, end, rings, send, recv, here):
        self.at, self.src, self.out = place, src, out
        self.held, self.twin, self.side, self.end, self.rings = held, twin, side, end, rings
        self.send, self.recv, self.here = send, recv, here

    def remote(self, k, src, dst, device):
        return pltpu.make_async_remote_copy(
            src_ref=src, dst_ref=dst, send_sem=self.send.at[k], recv_sem=self.recv.at[k],
            device_id=device, device_id_type=MESH)

    def load(self, k):
        a = self.at
        yx = (a.far, a.second, a.first, a.own)[k]
        return pltpu.make_async_copy(self.src.at[yx[0], a.c, :, yx[1]], self.held.at[k], self.here.at[k])

    def to_twin(self, k):
        a = self.at
        yx = (a.far, a.first, a.second, a.own)[k]
        return self.remote(k, self.src.at[yx[0], 1 - a.c, :, yx[1]], self.twin.at[k], a.to_sibling)

    def to_second(self, k):
        return self.remote(4 + k, self.held.at[k], self.side.at[k], self.at.to_second)

    def to_first(self):
        return self.remote(6, self.held.at[2], self.end, self.at.to_first)

    def ring(self, k):
        return self.remote(7 + k, self.held.at[3, self.at.chip(k + 1)], self.rings.at[k], self.at.to_next)

    def add(self, k, other):
        held = self.held

        def one(z, carry):
            total = held[k, z].astype(jnp.float32) + other[z].astype(jnp.float32)
            held[k, z] = total.astype(held.dtype)
            return carry

        lax.fori_loop(0, 4, one, 0)

    def stage(self, s):
        a = self.at
        if s == 0:
            for k in range(4):
                self.load(k).start()
                self.to_twin(k).start()
        elif s == 1:
            for k in range(2):
                self.load(k).wait()
                self.to_twin(k).wait_recv()
                self.add(k, self.twin.at[k])
                self.to_second(k).start()
        elif s == 2:
            for k in (2, 3):
                self.load(k).wait()
                self.to_twin(k).wait_recv()
                self.add(k, self.twin.at[k])
        elif s == 3:
            self.to_second(0).wait_recv()
            self.add(2, self.side.at[0])
            self.to_first().start()
        elif s == 4:
            self.to_second(1).wait_recv()
            self.add(3, self.side.at[1])
        elif s == 5:
            self.to_first().wait_recv()
            self.add(3, self.end)
            self.ring(0).start()
        elif s in (6, 7):
            self.ring(s - 6).wait_recv()
            z = a.chip(s - 4)
            total = self.held[3, z].astype(jnp.float32) + self.rings[s - 6].astype(jnp.float32)
            self.held[3, z] = total.astype(self.held.dtype)
            self.ring(s - 5).start()
        elif s == 8:
            self.ring(2).wait_recv()
            self.out[...] = self.held[3, a.z].astype(jnp.float32) + self.rings[2].astype(jnp.float32)

    def finish(self):
        for k in range(4):
            self.to_twin(k).wait_send()
        self.to_second(0).wait_send()
        self.to_second(1).wait_send()
        self.to_first().wait_send()
        for k in range(3):
            self.ring(k).wait_send()


def scatter_scratch(rows, cols, dtype):
    return [pltpu.VMEM((4, 4, rows, cols), dtype), pltpu.VMEM((4, 4, rows, cols), dtype),
            pltpu.VMEM((2, 4, rows, cols), dtype), pltpu.VMEM((4, rows, cols), dtype),
            pltpu.VMEM((3, rows, cols), dtype)]


def scatter_all(partials, offsets):
    n = len(partials)

    def body(*refs):
        src, out = refs[:n], refs[n:2 * n]
        scratch = refs[2 * n:7 * n]
        send, recv, here = refs[7 * n:]
        place = Place()
        place.greet()
        jobs = [Scatter(place, src[i], out[i], *scratch[5 * i:5 * i + 5], send.at[i], recv.at[i], here.at[i]) for i in range(n)]
        run_stages(jobs, offsets)

    scratch = []
    for p in partials:
        scratch += scatter_scratch(*p.shape[4:], p.dtype)
    return pl.pallas_call(
        body,
        out_shape=[jax.ShapeDtypeStruct(p.shape[4:], jnp.float32) for p in partials],
        in_specs=[pl.BlockSpec(memory_space=ANY)] * n,
        out_specs=[pl.BlockSpec(memory_space=pltpu.VMEM)] * n,
        scratch_shapes=scratch + [pltpu.SemaphoreType.DMA((n, 10)), pltpu.SemaphoreType.DMA((n, 10)), pltpu.SemaphoreType.DMA((n, 4))],
        compiler_params=pltpu.CompilerParams(collective_id=1, has_side_effects=True, vmem_limit_bytes=50 << 20),
        name="scatter_grads",
    )(*partials)


STEP = 544
KEYS = 640
NEGATIVE = -1e30
F32 = jnp.float32
LOW = jnp.bfloat16
VMEM = pltpu.VMEM


def dot(a, b):
    return lax.dot_general(a, b, (((1,), (0,)), ((), ())), preferred_element_type=F32)


def dot_t(a, b):
    return lax.dot_general(a, b, (((1,), (1,)), ((), ())), preferred_element_type=F32)


def lanes_of(shape):
    return lax.broadcasted_iota(jnp.int32, shape, 1)


def standard(rows):
    width = rows.shape[-1]
    centred = rows - jnp.sum(rows, axis=-1, keepdims=True) * (1.0 / width)
    spread = jnp.sum(centred * centred, axis=-1, keepdims=True) * (1.0 / width)
    inverse = lax.rsqrt(spread + epsilon)
    return centred * inverse, inverse


def standard_back(normed, inverse, e):
    width = e.shape[-1]
    mean_e = jnp.sum(e, axis=-1, keepdims=True) * (1.0 / width)
    mean_en = jnp.sum(e * normed, axis=-1, keepdims=True) * (1.0 / width)
    return (e - mean_e - normed * mean_en) * inverse


def first_norm(x_ref, vec_ref, hn_ref, hnt_ref):
    tokens = x_ref.shape[0]
    tile = 128

    def one(i, carry):
        rows = pl.ds(pl.multiple_of(i * tile, tile), tile)
        n, _ = standard(x_ref[rows, :].astype(F32))
        hn = (n * vec_ref[0:1, :] + vec_ref[1:2, :]).astype(LOW)
        hn_ref[rows, :] = hn
        hnt_ref[:, rows] = hn.T
        return carry

    whole = tokens // tile
    lax.fori_loop(0, whole, one, 0)
    rest = tokens - whole * tile
    n, _ = standard(x_ref[whole * tile :, :].astype(F32))
    hn = (n * vec_ref[0:1, :] + vec_ref[1:2, :]).astype(LOW)
    hn_ref[whole * tile :, :] = hn
    padded = jnp.concatenate([hn, jnp.zeros((tile - rest, hn.shape[1]), LOW)], axis=0)
    hnt_ref[:, whole * tile :] = padded.T


def project_qkv(hn_ref, w_ref, bias_ref, qkv_ref):
    tokens, columns = hn_ref.shape[0], 256
    n = w_ref.shape[1] // columns
    qkv_ref[tokens:, :] = jnp.zeros((qkv_ref.shape[0] - tokens, qkv_ref.shape[1]), LOW)

    def one(j, carry):
        cols = pl.ds(pl.multiple_of(j * columns, columns), columns)
        bias = bias_ref[0:1, cols]
        weight = w_ref[:, cols]
        for b in range(tokens // STEP):
            rows = slice(b * STEP, (b + 1) * STEP)
            qkv_ref[rows, cols] = (dot(hn_ref[rows, :], weight) + bias).astype(LOW)
        return carry

    lax.fori_loop(0, n, one, 0)


def attend(b, pair, qkv_ref, augk_ref, o_ref, augq_ref, width):
    base = pl.multiple_of(b * STEP, STEP)
    lane = pl.multiple_of(pair * 128, 128)
    q = qkv_ref[pl.ds(base, STEP), pl.ds(lane, 128)]
    k = qkv_ref[pl.ds(base, KEYS), pl.ds(width + lane, 128)]
    v = qkv_ref[pl.ds(base, KEYS), pl.ds(2 * width + lane, 128)]
    augk = augk_ref[b]
    half_q = lanes_of(q.shape) < 64
    half_k = lanes_of(k.shape) < 64
    start = jnp.where(lanes_of(q.shape) % 64 == 0, 1.0, 0.0).astype(LOW)
    ones = jnp.ones(v.shape, LOW)
    peaks, outs = [], []
    for h in range(2):
        side_q = half_q if h == 0 else ~half_q
        side_k = half_k if h == 0 else ~half_k
        raw = dot_t(jnp.where(side_q, q, start), jnp.where(side_k, k, augk))
        peak = jnp.max(raw, axis=-1, keepdims=True)
        p = jnp.exp((raw - peak) * 0.125).astype(LOW)
        outs.append(dot(p, jnp.where(side_k, v, ones)))
        peaks.append(peak)
    half = lanes_of(outs[0].shape) < 64
    data = jnp.where(half, outs[0], outs[1])
    total_other = jnp.where(half, outs[1], outs[0])
    total = pltpu.roll(total_other, 64, 1)
    o_ref[pl.ds(base, STEP), pl.ds(lane, 128)] = (data / total).astype(LOW)
    level = jnp.where(half, peaks[1], peaks[0]) + 8.0 * jnp.log(total_other)
    high = level.astype(LOW)
    rest = level - high.astype(F32)
    mid = rest.astype(LOW)
    last = (rest - mid.astype(F32)).astype(LOW)
    spot = lanes_of(high.shape) % 64
    zero = jnp.zeros_like(high)
    aug = jnp.where(spot == 0, jnp.ones_like(high),
          jnp.where(spot == 1, -high, jnp.where(spot == 2, -mid, jnp.where(spot == 3, -last, zero))))
    slot = b * (width // 128) + pair
    augq_ref[slot, 0:STEP, :] = aug
    tail = (KEYS - STEP, 128)
    augq_ref[slot, STEP:KEYS, :] = jnp.where(lanes_of(tail) % 64 == 1, NEGATIVE, 0.0).astype(LOW)


def attend_back(b, pair, qkv_ref, augk_ref, augq_ref, do_ref, o_ref, dqkv_ref, width):
    base = pl.multiple_of(b * STEP, STEP)
    lane = pl.multiple_of(pair * 128, 128)
    wide, rows, cols = pl.ds(base, KEYS), pl.ds(base, STEP), pl.ds(lane, 128)
    q = qkv_ref[wide, cols]
    k = qkv_ref[rows, pl.ds(width + lane, 128)]
    v = qkv_ref[rows, pl.ds(2 * width + lane, 128)]
    do = do_ref[wide, cols]
    augq = augq_ref[b * (width // 128) + pair]
    augk = augk_ref[b, 0:STEP, :]
    shape_q, shape_k = (KEYS, 128), (STEP, 128)
    prod = do.astype(F32) * o_ref[wide, cols].astype(F32)
    high = prod.astype(LOW)
    mid = (prod - high.astype(F32)).astype(LOW)
    swap = ((lax.broadcasted_iota(jnp.int32, (128, 128), 0) < 64) != (lanes_of((128, 128)) < 64)).astype(F32).astype(LOW)
    delta = dot(high, swap) + dot(mid, swap)
    high = delta.astype(LOW)
    mid = (delta - high.astype(F32)).astype(LOW)
    spot = lanes_of(shape_q) % 64
    augdo = jnp.where(spot == 0, -high, jnp.where(spot == 1, -mid, jnp.zeros_like(high)))
    augv = jnp.where(lanes_of(shape_k) % 64 < 2, 1.0, 0.0).astype(LOW)
    half_q, half_k = lanes_of(shape_q) < 64, lanes_of(shape_k) < 64
    kt = k.T
    dks, dvs, dqs = [], [], []
    for h in range(2):
        side_q = half_q if h == 0 else ~half_q
        side_k = half_k if h == 0 else ~half_k
        raw = dot_t(jnp.where(side_k, k, augk), jnp.where(side_q, q, augq))
        p = jnp.exp(raw * 0.125)
        dp = dot_t(jnp.where(side_k, v, augv), jnp.where(side_q, do, augdo))
        ds = (p * dp).astype(LOW)
        dvs.append(dot(p.astype(LOW), do))
        dks.append(dot(ds, q))
        dqs.append(dot(kt, ds))
    dqt = jnp.concatenate([dqs[0][:64], dqs[1][64:]], axis=0) * 0.125
    dqkv_ref[rows, cols] = dqt.T[0:STEP, :].astype(LOW)
    dqkv_ref[rows, pl.ds(width + lane, 128)] = (jnp.where(half_k, dks[0], dks[1]) * 0.125).astype(LOW)
    dqkv_ref[rows, pl.ds(2 * width + lane, 128)] = jnp.where(half_k, dvs[0], dvs[1]).astype(LOW)


def project_out(o_ref, w_ref, x_ref, vec_ref, r_ref, ot_ref):
    tokens = x_ref.shape[0]
    for b in range(tokens // STEP):
        rows = slice(b * STEP, (b + 1) * STEP)
        r_ref[rows, :] = x_ref[rows, :].astype(F32) + (dot(o_ref[rows, :], w_ref[...]) + vec_ref[4:5, :])
    tile = 128

    def one(i, carry):
        rows = pl.ds(pl.multiple_of(i * tile, tile), tile)
        ot_ref[:, rows] = o_ref[rows, :].T
        return carry

    lax.fori_loop(0, ot_ref.shape[1] // tile, one, 0)


def forward_body(x_ref, vec_ref, bias_ref, wq_ref, wp_ref, augk_ref, qkv_ref, o_ref, augq_ref, r_ref, hnt_ref, ot_ref, hn_ref):
    width = x_ref.shape[1]
    tokens = x_ref.shape[0]
    first_norm(x_ref, vec_ref, hn_ref, hnt_ref)
    project_qkv(hn_ref, wq_ref, bias_ref, qkv_ref)
    o_ref[tokens:, :] = jnp.zeros((o_ref.shape[0] - tokens, width), LOW)
    pairs = width // 128

    def one(i, carry):
        attend(i // pairs, i % pairs, qkv_ref, augk_ref, o_ref, augq_ref, width)
        return carry

    lax.fori_loop(0, pairs * (tokens // STEP), one, 0)
    project_out(o_ref, wp_ref, x_ref, vec_ref, r_ref, ot_ref)


def sizes(tokens):
    tall = tokens + KEYS - STEP
    even = -(-tokens // 128) * 128
    return tall, even


def forward_attention(x, vec, bias, wq, wp, augk):
    tokens, width = x.shape
    tall, even = sizes(tokens)
    items = tokens // STEP
    out = [((tall, 3 * width), LOW), ((tall, width), LOW), ((items * (width // 128), KEYS, 128), LOW),
           ((tokens, width), F32), ((width, even), LOW), ((width, even), LOW)]
    return pl.pallas_call(
        forward_body,
        out_shape=[jax.ShapeDtypeStruct(s, d) for s, d in out],
        in_specs=[pl.BlockSpec(memory_space=VMEM)] * 6,
        out_specs=[pl.BlockSpec(memory_space=VMEM)] * 6,
        scratch_shapes=[pltpu.VMEM((tokens, width), LOW)],
        compiler_params=pltpu.CompilerParams(vmem_limit_bytes=58 << 20),
        name="forward_attention",
    )(x, vec, bias, wq, wp, augk)


ERFC = (-0.028961464762687683, 0.13991104066371918, -0.23952563107013702, 0.13530659675598145, -0.011358031071722507, 0.10075884312391281, 0.12164358794689178, 0.14118188619613647, 0.14104320108890533)


def gelu_parts(u):
    t = pl.reciprocal(1.0 + (0.5 * 0.5 ** 0.5) * jnp.abs(u), approx=False)
    poly = jnp.full_like(t, ERFC[0])
    for c in ERFC[1:]:
        poly = poly * t + c
    bell = jnp.exp(-0.5 * (u * u))
    tail = poly * t * bell
    phi = jnp.where(u >= 0, 1.0 - tail, tail)
    return u * phi, phi + u * (bell * 0.3989422804014327)


def mlp_body(chunk, r_ref, dy_ref, vec_ref, up_bias_ref, wu_ref, wd_ref,
             out_ref, dr_ref, sums_ref, gub_ref, gwu_ref, gwd_ref,
             hm_ref, hmt_ref, m_ref, dhm_ref, du_ref):
    step = pl.program_id(0)
    steps = pl.num_programs(0)
    tokens, width = r_ref.shape
    even = hmt_ref.shape[1]
    tile = 128
    whole = tokens // tile

    @pl.when(step == 0)
    def _():
        def one(i, carry):
            rows = pl.ds(pl.multiple_of(i * tile, tile), tile)
            n, _ = standard(r_ref[rows, :])
            hm = (n * vec_ref[5:6, :] + vec_ref[6:7, :]).astype(LOW)
            hm_ref[rows, :] = hm
            hmt_ref[:, rows] = hm.T
            return carry

        lax.fori_loop(0, whole, one, 0)
        n, _ = standard(r_ref[whole * tile :, :])
        hm = (n * vec_ref[5:6, :] + vec_ref[6:7, :]).astype(LOW)
        hm_ref[whole * tile :, :] = hm
        rest = jnp.zeros((even - tokens, width), LOW)
        hmt_ref[:, whole * tile :] = jnp.concatenate([hm, rest], axis=0).T
        du_ref[tokens:, :] = jnp.zeros((even - tokens, chunk), LOW)
        m_ref[...] = jnp.zeros_like(m_ref)
        dhm_ref[...] = jnp.zeros_like(dhm_ref)

    bias = up_bias_ref[0:1, :]
    for b in range(tokens // STEP):
        rows = slice(b * STEP, (b + 1) * STEP)
        u = dot(hm_ref[rows, :], wu_ref[...]) + bias
        gl, slope = gelu_parts(u)
        gl = gl.astype(LOW)
        dm = dy_ref[rows, :]
        du = (dot_t(dm, wd_ref[...]) * slope).astype(LOW)
        du_ref[rows, :] = du
        m_ref[rows, :] += dot(gl, wd_ref[...])
        dhm_ref[rows, :] += dot_t(du, wu_ref[...])
        total = jnp.sum(du.astype(F32), axis=0, keepdims=True)
        part = lax.dot_general(gl, dm, (((0,), (0,)), ((), ())), preferred_element_type=F32)
        if b == 0:
            ub_sum, down = total, part
        else:
            ub_sum, down = ub_sum + total, down + part
    gub_ref[...] = jnp.broadcast_to(ub_sum, gub_ref.shape)
    gwd_ref[...] = down.astype(LOW)
    gwu_ref[...] = dot(hmt_ref[...], du_ref[...]).astype(LOW)

    @pl.when(step == steps - 1)
    def _():
        sums_ref[...] = jnp.zeros_like(sums_ref)

        def back(rows):
            r = r_ref[rows, :]
            n, inverse = standard(r)
            dy = dy_ref[rows, :].astype(F32)
            dhm = dhm_ref[rows, :]
            out_ref[rows, :] = (r + (m_ref[rows, :] + vec_ref[7:8, :])).astype(LOW)
            dr_ref[rows, :] = dy + standard_back(n, inverse, dhm * vec_ref[5:6, :])
            sums_ref[0:1, :] += jnp.sum(dhm * n, axis=0, keepdims=True)
            sums_ref[1:2, :] += jnp.sum(dhm, axis=0, keepdims=True)
            sums_ref[2:3, :] += jnp.sum(dy, axis=0, keepdims=True)

        def one(i, carry):
            back(pl.ds(pl.multiple_of(i * 64, 64), 64))
            return carry

        lax.fori_loop(0, tokens // 64, one, 0)


def feed_forward(r, dy, vec, up_bias, wu, wd, chunk=512):
    tokens, width = r.shape
    hidden = wu.shape[1]
    _, even = sizes(tokens)
    whole = lambda *s: pl.BlockSpec(s, lambda j: (0,) * len(s))
    return pl.pallas_call(
        functools.partial(mlp_body, chunk),
        grid=(hidden // chunk,),
        out_shape=[jax.ShapeDtypeStruct((tokens, width), LOW), jax.ShapeDtypeStruct((tokens, width), F32),
                   jax.ShapeDtypeStruct((8, width), F32), jax.ShapeDtypeStruct((8, hidden), F32),
                   jax.ShapeDtypeStruct((width, hidden), LOW), jax.ShapeDtypeStruct((hidden, width), LOW)],
        in_specs=[whole(tokens, width), whole(tokens, width), whole(8, width),
                  pl.BlockSpec((8, chunk), lambda j: (0, j)),
                  pl.BlockSpec((width, chunk), lambda j: (0, j)),
                  pl.BlockSpec((chunk, width), lambda j: (j, 0))],
        out_specs=[whole(tokens, width), whole(tokens, width), whole(8, width),
                   pl.BlockSpec((8, chunk), lambda j: (0, j)),
                   pl.BlockSpec((width, chunk), lambda j: (0, j)),
                   pl.BlockSpec((chunk, width), lambda j: (j, 0))],
        scratch_shapes=[pltpu.VMEM((tokens, width), LOW), pltpu.VMEM((width, even), LOW),
                        pltpu.VMEM((tokens, width), F32), pltpu.VMEM((tokens, width), F32),
                        pltpu.VMEM((even, chunk), LOW)],
        compiler_params=pltpu.CompilerParams(vmem_limit_bytes=58 << 20),
        name="feed_forward",
    )(r, dy, vec, up_bias, wu, wd)


def backward_body(x_ref, vec_ref, wq_ref, wp_ref, augk_ref, qkv_ref, o_ref, augq_ref, hnt_ref, ot_ref, dr_ref,
                  dx_ref, gwq_ref, gwp_ref, sums_ref, gqb_ref, do_ref, da_ref, dqkv_ref):
    tokens, width = x_ref.shape
    pairs = width // 128
    items = tokens // STEP
    even = hnt_ref.shape[1]
    da_ref[tokens:, :] = jnp.zeros((even - tokens, width), LOW)
    do_ref[tokens:, :] = jnp.zeros((do_ref.shape[0] - tokens, width), LOW)
    dqkv_ref[tokens:, :] = jnp.zeros((even - tokens, 3 * width), LOW)
    sums_ref[...] = jnp.zeros_like(sums_ref)
    for b in range(items):
        rows = slice(b * STEP, (b + 1) * STEP)
        da = dr_ref[rows, :].astype(LOW)
        da_ref[rows, :] = da
        sums_ref[0:1, :] += jnp.sum(da.astype(F32), axis=0, keepdims=True)
        do_ref[rows, :] = dot_t(da, wp_ref[...]).astype(LOW)
    gwp_ref[...] = dot(ot_ref[...], da_ref[...]).astype(LOW)

    def group(g, carry):
        def one(i, carry):
            attend_back(i // 2, g * 2 + i % 2, qkv_ref, augk_ref, augq_ref, do_ref, o_ref, dqkv_ref, width)
            return carry

        lax.fori_loop(0, 2 * items, one, 0)
        for part in range(3):
            cols = pl.ds(pl.multiple_of(part * width + g * 256, 256), 256)
            d = dqkv_ref[:, cols]
            gwq_ref[:, cols] = dot(hnt_ref[...], d).astype(LOW)
            gqb_ref[:, cols] = jnp.broadcast_to(jnp.sum(d.astype(F32), axis=0, keepdims=True), (8, 256))
        return carry

    lax.fori_loop(0, pairs // 2, group, 0)
    for b in range(items):
        rows = slice(b * STEP, (b + 1) * STEP)
        dhn = dot_t(dqkv_ref[rows, :], wq_ref[...])
        n, inverse = standard(x_ref[rows, :].astype(F32))
        dx = dr_ref[rows, :] + standard_back(n, inverse, dhn * vec_ref[0:1, :])
        dx_ref[rows, :] = dx.astype(LOW)
        sums_ref[1:2, :] += jnp.sum(dhn * n, axis=0, keepdims=True)
        sums_ref[2:3, :] += jnp.sum(dhn, axis=0, keepdims=True)


def backward_attention(x, vec, wq, wp, augk, qkv, o, augq, hnt, ot, dr):
    tokens, width = x.shape
    tall, even = sizes(tokens)
    return pl.pallas_call(
        backward_body,
        out_shape=[jax.ShapeDtypeStruct((tokens, width), LOW), jax.ShapeDtypeStruct((width, 3 * width), LOW),
                   jax.ShapeDtypeStruct((width, width), LOW), jax.ShapeDtypeStruct((8, width), F32),
                   jax.ShapeDtypeStruct((8, 3 * width), F32)],
        in_specs=[pl.BlockSpec(memory_space=VMEM)] * 11,
        out_specs=[pl.BlockSpec(memory_space=VMEM)] * 5,
        scratch_shapes=[pltpu.VMEM((tall, width), LOW), pltpu.VMEM((even, width), LOW), pltpu.VMEM((even, 3 * width), LOW)],
        compiler_params=pltpu.CompilerParams(vmem_limit_bytes=60 << 20),
        name="backward_attention",
    )(x, vec, wq, wp, augk, qkv, o, augq, hnt, ot, dr)


def pack_vectors(eight, wide):
    block = jnp.stack(eight, axis=-2)
    rows = wide.reshape(wide.shape[:-1] + (4, -1))
    lead = [(0, 0)] * (block.ndim - 2)
    rows = jnp.pad(rows, lead + [(0, 4), (0, 0)])
    joined = jnp.concatenate([block, rows], axis=-1)
    return jnp.pad(joined, lead + [(0, 0), (0, 128 - joined.shape[-1])])


def unpack_vectors(blocks, share):
    eight = tuple(blocks[:, k, :share].reshape(-1) for k in range(8))
    return eight, blocks[:, :4, share : 2 * share].reshape(-1)


def pad_rows(rows, items, length, step):
    parts = rows.reshape(items, length, -1)
    return jnp.pad(parts, ((0, 0), (0, step - length), (0, 0))).reshape(items * step, -1)


def local(
    patches,
    cotangent,
    counts,
    blank_mask,
    ln1_gain,
    ln1_shift,
    w_qkv,
    query_bias,
    value_bias,
    w_proj,
    proj_bias,
    ln2_gain,
    ln2_shift,
    w_up,
    up_bias,
    w_down,
    down_bias,
):
    items, length = blank_mask.shape
    width = patches.shape[1]
    share = w_qkv.shape[0]
    positions = jnp.arange(length, dtype=jnp.int32)
    live = positions[None, :] < counts[:, None]
    allowed = live & ((blank_mask == 1) | (positions[None, :] == 0))
    bias = jnp.where(allowed, 0.0, NEGATIVE)
    bias = jnp.pad(bias, ((0, 0), (0, KEYS - length)), constant_values=NEGATIVE)
    spot = jnp.arange(128) % HEAD_DIM
    augk = jnp.where(spot == 0, bias[:, :, None], jnp.where(spot < 4, 1.0, 0.0)).astype(LOW)
    x = pad_rows(patches, items, length, STEP)
    dy = pad_rows(jnp.where(live.reshape(-1, 1), cotangent, 0), items, length, STEP)
    vectors = pack_vectors(
        (ln1_gain, ln1_shift, query_bias, value_bias, proj_bias, ln2_gain, ln2_shift, down_bias),
        up_bias,
    )
    all_qkv, all_vectors, all_proj, all_up, all_down = gather_all(
        (w_qkv, vectors, w_proj, w_up, w_down), (0, 0, 3, 4, 7)
    )
    wq = all_qkv.reshape(width, -1)
    wp = all_proj.reshape(width, width)
    wu = all_up.reshape(width, -1)
    wd = all_down.reshape(-1, width)
    eight, up = unpack_vectors(all_vectors.reshape(-1, 8, 128).astype(F32), share)
    vec = jnp.stack(eight)
    qkv_bias = jnp.broadcast_to(
        jnp.concatenate([eight[2], jnp.zeros_like(eight[2]), eight[3]])[None], (8, 3 * width)
    )
    qkv, o, augq, r, hnt, ot = forward_attention(x, vec, qkv_bias, wq, wp, augk)
    out, dr, sums_mlp, gub, gwu, gwd = feed_forward(
        r, dy, vec, jnp.broadcast_to(up[None], (8, up.shape[0])), wu, wd
    )
    dx, gwq, gwp, sums_attn, gqb = backward_attention(x, vec, wq, wp, augk, qkv, o, augq, hnt, ot, dr)
    gains = (
        sums_attn[1],
        sums_attn[2],
        gqb[0, :width],
        gqb[0, 2 * width :],
        sums_attn[0],
        sums_mlp[0],
        sums_mlp[1],
        sums_mlp[2],
    )
    packed = pack_vectors(tuple(v.reshape(-1, share) for v in gains), gub[0].reshape(-1, 4 * share))
    blocks = tuple(
        t.reshape((2, 2, 4, 2) + s)
        for t, s in (
            (gwd, w_down.shape),
            (gwu, w_up.shape),
            (gwp, w_proj.shape),
            (gwq, w_qkv.shape),
            (packed, (8, 128)),
        )
    )
    own_down, own_up, own_proj, own_qkv, own_packed = scatter_all(blocks, (0, 3, 6, 7, 8))
    own, own_up_bias = unpack_vectors(own_packed[None], share)

    def unpad(rows):
        return rows.reshape(items, STEP, width)[:, :length].reshape(items * length, width)

    output = jnp.where(live.reshape(-1, 1), unpad(out), 0)
    return (
        output,
        unpad(dx),
        own[0],
        own[1],
        own_qkv,
        own[2],
        own[3],
        own_proj,
        own[4],
        own[5],
        own[6],
        own_up,
        own_up_bias,
        own_down,
        own[7],
    )


def plain_local(
    patches,
    cotangent,
    counts,
    blank_mask,
    ln1_gain,
    ln1_shift,
    w_qkv,
    query_bias,
    value_bias,
    w_proj,
    proj_bias,
    ln2_gain,
    ln2_shift,
    w_up,
    up_bias,
    w_down,
    down_bias,
):
    items_here = counts.shape[0]
    length = blank_mask.shape[1]
    width = patches.shape[1]
    positions = jnp.arange(length, dtype=jnp.int32)
    live_mask = positions[None, :] < counts[:, None]
    allowed = live_mask & ((blank_mask == 1) | (positions[None, :] == 0))
    live_rows = live_mask.reshape(-1, 1).astype(jnp.float32)
    attn_full = (
        lax.all_gather(ln1_gain, ("gx", "gy"), axis=0, tiled=True),
        lax.all_gather(ln1_shift, ("gx", "gy"), axis=0, tiled=True),
        lax.all_gather(w_qkv, ("gx", "gy"), axis=0, tiled=True),
        lax.all_gather(query_bias, ("gx", "gy"), axis=0, tiled=True),
        lax.all_gather(value_bias, ("gx", "gy"), axis=0, tiled=True),
        lax.all_gather(w_proj, ("gx", "gy"), axis=0, tiled=True),
        lax.all_gather(proj_bias, ("gx", "gy"), axis=0, tiled=True),
    )
    gain_one, shift_one, qkv_weight, bias_query, bias_value, proj_weight, bias_proj = attn_full
    inputs = patches.astype(jnp.float32)
    gain_float = gain_one.astype(jnp.float32)
    shift_float = shift_one.astype(jnp.float32)
    normed_low = normalize(inputs, gain_float, shift_float).astype(jnp.bfloat16)
    projected = jnp.dot(normed_low, qkv_weight, preferred_element_type=jnp.float32)
    queries = (projected[:, :width] + bias_query.astype(jnp.float32)).astype(jnp.bfloat16)
    keys_all = projected[:, width : 2 * width].astype(jnp.bfloat16)
    values_all = (projected[:, 2 * width :] + bias_value.astype(jnp.float32)).astype(jnp.bfloat16)
    per_item = (
        queries.reshape(items_here, length, width),
        keys_all.reshape(items_here, length, width),
        values_all.reshape(items_here, length, width),
        allowed,
    )
    mixed_items, log_totals = lax.map(attend_forward, per_item)
    mixed_low = mixed_items.reshape(-1, width)
    residual = (
        inputs
        + jnp.dot(mixed_low, proj_weight, preferred_element_type=jnp.float32)
        + bias_proj.astype(jnp.float32)
    )
    mlp_full = (
        lax.all_gather(ln2_gain, ("gx", "gy"), axis=0, tiled=True),
        lax.all_gather(ln2_shift, ("gx", "gy"), axis=0, tiled=True),
        lax.all_gather(w_up, ("gx", "gy"), axis=0, tiled=True),
        lax.all_gather(up_bias, ("gx", "gy"), axis=0, tiled=True),
        lax.all_gather(w_down, ("gx", "gy"), axis=0, tiled=True),
        lax.all_gather(down_bias, ("gx", "gy"), axis=0, tiled=True),
    )
    gain_two, shift_two, up_weight, bias_up, down_weight, bias_down = mlp_full
    normed_two = normalize(
        residual, gain_two.astype(jnp.float32), shift_two.astype(jnp.float32)
    ).astype(jnp.bfloat16)
    pre_act = jnp.dot(normed_two, up_weight, preferred_element_type=jnp.float32) + bias_up.astype(
        jnp.float32
    )
    activated, gelu_back = jax.vjp(partial(jax.nn.gelu, approximate=False), pre_act)
    act_low = activated.astype(jnp.bfloat16)
    out_branch = jnp.dot(
        act_low, down_weight, preferred_element_type=jnp.float32
    ) + bias_down.astype(jnp.float32)
    output = ((residual + out_branch) * live_rows).astype(jnp.bfloat16)
    mlp_back = (
        lax.all_gather(ln2_gain, ("gx", "gy"), axis=0, tiled=True),
        lax.all_gather(ln2_shift, ("gx", "gy"), axis=0, tiled=True),
        lax.all_gather(w_up, ("gx", "gy"), axis=0, tiled=True),
        lax.all_gather(up_bias, ("gx", "gy"), axis=0, tiled=True),
        lax.all_gather(w_down, ("gx", "gy"), axis=0, tiled=True),
        lax.all_gather(down_bias, ("gx", "gy"), axis=0, tiled=True),
    )
    gain_two_b, shift_two_b, up_weight_b, bias_up_b, down_weight_b, bias_down_b = mlp_back
    grad_out = cotangent.astype(jnp.float32) * live_rows
    grad_down_low = grad_out.astype(jnp.bfloat16)
    down_grad = jnp.einsum("tf,td->fd", act_low, grad_down_low, preferred_element_type=jnp.float32)
    down_bias_grad = jnp.sum(grad_down_low.astype(jnp.float32), axis=0)
    grad_act = jnp.einsum(
        "td,fd->tf", grad_down_low, down_weight_b, preferred_element_type=jnp.float32
    )
    grad_pre_low = gelu_back(grad_act)[0].astype(jnp.bfloat16)
    up_grad = jnp.einsum("td,tf->df", normed_two, grad_pre_low, preferred_element_type=jnp.float32)
    up_bias_grad = jnp.sum(grad_pre_low.astype(jnp.float32), axis=0)
    grad_normed_two = jnp.einsum(
        "tf,df->td", grad_pre_low, up_weight_b, preferred_element_type=jnp.float32
    )
    _, norm_back_two = jax.vjp(
        normalize, residual, gain_two_b.astype(jnp.float32), shift_two_b.astype(jnp.float32)
    )
    grad_resid_part, gain_two_grad, shift_two_grad = norm_back_two(grad_normed_two)
    grad_resid = grad_out + grad_resid_part
    mlp_owned = (
        lax.psum_scatter(gain_two_grad, ("gx", "gy"), scatter_dimension=0, tiled=True),
        lax.psum_scatter(shift_two_grad, ("gx", "gy"), scatter_dimension=0, tiled=True),
        lax.psum_scatter(up_grad, ("gx", "gy"), scatter_dimension=0, tiled=True),
        lax.psum_scatter(up_bias_grad, ("gx", "gy"), scatter_dimension=0, tiled=True),
        lax.psum_scatter(down_grad, ("gx", "gy"), scatter_dimension=0, tiled=True),
        lax.psum_scatter(down_bias_grad, ("gx", "gy"), scatter_dimension=0, tiled=True),
    )
    attn_back = (
        lax.all_gather(ln1_gain, ("gx", "gy"), axis=0, tiled=True),
        lax.all_gather(ln1_shift, ("gx", "gy"), axis=0, tiled=True),
        lax.all_gather(w_qkv, ("gx", "gy"), axis=0, tiled=True),
        lax.all_gather(query_bias, ("gx", "gy"), axis=0, tiled=True),
        lax.all_gather(value_bias, ("gx", "gy"), axis=0, tiled=True),
        lax.all_gather(w_proj, ("gx", "gy"), axis=0, tiled=True),
        lax.all_gather(proj_bias, ("gx", "gy"), axis=0, tiled=True),
    )
    (
        gain_one_b,
        shift_one_b,
        qkv_weight_b,
        bias_query_b,
        bias_value_b,
        proj_weight_b,
        bias_proj_b,
    ) = attn_back
    grad_branch_low = grad_resid.astype(jnp.bfloat16)
    proj_grad = jnp.einsum(
        "td,te->de", mixed_low, grad_branch_low, preferred_element_type=jnp.float32
    )
    proj_bias_grad = jnp.sum(grad_branch_low.astype(jnp.float32), axis=0)
    grad_mixed = jnp.einsum(
        "te,de->td", grad_branch_low, proj_weight_b, preferred_element_type=jnp.float32
    ).astype(jnp.bfloat16)
    back_items = (
        per_item[0],
        per_item[1],
        per_item[2],
        allowed,
        log_totals,
        grad_mixed.reshape(items_here, length, width),
    )
    grad_projected = lax.map(attend_backward, back_items).reshape(-1, 3 * width)
    qkv_grad = jnp.einsum(
        "td,te->de", normed_low, grad_projected, preferred_element_type=jnp.float32
    )
    query_bias_grad = jnp.sum(grad_projected[:, :width].astype(jnp.float32), axis=0)
    value_bias_grad = jnp.sum(grad_projected[:, 2 * width :].astype(jnp.float32), axis=0)
    grad_normed = jnp.einsum(
        "te,de->td", grad_projected, qkv_weight_b, preferred_element_type=jnp.float32
    )
    _, norm_back_one = jax.vjp(
        normalize, inputs, gain_one_b.astype(jnp.float32), shift_one_b.astype(jnp.float32)
    )
    grad_input_part, gain_one_grad, shift_one_grad = norm_back_one(grad_normed)
    grad_input = (grad_resid + grad_input_part).astype(jnp.bfloat16)
    attn_owned = (
        lax.psum_scatter(gain_one_grad, ("gx", "gy"), scatter_dimension=0, tiled=True),
        lax.psum_scatter(shift_one_grad, ("gx", "gy"), scatter_dimension=0, tiled=True),
        lax.psum_scatter(qkv_grad, ("gx", "gy"), scatter_dimension=0, tiled=True),
        lax.psum_scatter(query_bias_grad, ("gx", "gy"), scatter_dimension=0, tiled=True),
        lax.psum_scatter(value_bias_grad, ("gx", "gy"), scatter_dimension=0, tiled=True),
        lax.psum_scatter(proj_grad, ("gx", "gy"), scatter_dimension=0, tiled=True),
        lax.psum_scatter(proj_bias_grad, ("gx", "gy"), scatter_dimension=0, tiled=True),
    )
    owned_all = attn_owned + mlp_owned
    return (
        output,
        grad_input,
        owned_all[0],
        owned_all[1],
        owned_all[2],
        owned_all[3],
        owned_all[4],
        owned_all[5],
        owned_all[6],
        owned_all[7],
        owned_all[8],
        owned_all[9],
        owned_all[10],
        owned_all[11],
        owned_all[12],
    )


def solution(mesh):
    placed = (
        P(("gx", "gy"), None),
        P(("gx", "gy"), None),
        P(("gx", "gy")),
        P(("gx", "gy"), None),
        P(("gx", "gy")),
        P(("gx", "gy")),
        P(("gx", "gy"), None),
        P(("gx", "gy")),
        P(("gx", "gy")),
        P(("gx", "gy"), None),
        P(("gx", "gy")),
        P(("gx", "gy")),
        P(("gx", "gy")),
        P(("gx", "gy"), None),
        P(("gx", "gy")),
        P(("gx", "gy"), None),
        P(("gx", "gy")),
    )
    mine = dict(mesh.shape) == {"gx": 4, "gy": 8}
    return jax.shard_map(
        local if mine else plain_local,
        mesh=mesh,
        in_specs=placed,
        out_specs=(
            P(("gx", "gy"), None),
            P(("gx", "gy"), None),
            P(("gx", "gy")),
            P(("gx", "gy")),
            P(("gx", "gy"), None),
            P(("gx", "gy")),
            P(("gx", "gy")),
            P(("gx", "gy"), None),
            P(("gx", "gy")),
            P(("gx", "gy")),
            P(("gx", "gy")),
            P(("gx", "gy"), None),
            P(("gx", "gy")),
            P(("gx", "gy"), None),
            P(("gx", "gy")),
        ),
        check_vma=False,
    )
```
